128 devices in a mesh: seq: 32 (over y, z, core), tp: 4 (over x).
Axes of the slice: x: 4, y: 4, z: 4, core: 2. Of those that a mesh axis runs over, the one named last changes fastest.
Arguments:
- hidden_cat: bfloat16 [16384, 7168], P('seq'), may hold values from -6 to 6
- norm_gain: float32 [7168], replicated, may hold values from 0.5 to 1.5
- k_weight: bfloat16 [7168, 3584], P('seq', 'tp'), may hold values from -0.0625 to 0.0625
- v_weight: bfloat16 [7168, 3584], P('seq', 'tp'), may hold values from -0.0625 to 0.0625
- k_down: bfloat16 [7168, 128], P('seq'), may hold values from -0.0625 to 0.0625
- v_down: bfloat16 [7168, 128], P('seq'), may hold values from -0.0625 to 0.0625
- k_up: bfloat16 [128, 3584], P(None, 'tp'), may hold values from -0.23925781 to 0.23925781
- v_up: bfloat16 [128, 3584], P(None, 'tp'), may hold values from -0.23925781 to 0.23925781
- queries: bfloat16 [16384, 3584], P('seq', 'tp')
- o_weight: bfloat16 [3584, 3584], P('tp'), may hold values from -0.09375 to 0.09375
- final_gain: float32 [3584], replicated, may hold values from 0.5 to 1.5
- unembed: bfloat16 [32000, 3584], P(('seq', 'tp')), may hold values from -0.29882812 to 0.29882812
- lengths: int32 [12], replicated, may hold values from 1 to 2048, 16384 in all
- req_prompt: int32 [16], replicated, may hold values from 0 to 11
- page_owner: int32 [2048], P('seq'), may hold values from 0 to 31, as said below
Outputs:
- attended: bfloat16 [16384, 3584], P('seq', 'tp')
- kv_cache: bfloat16 [2048, 8, 2, 3584], P('seq', None, None, 'tp')
- state_norm: float32 [16], replicated
- logit_max: float32 [16], replicated
The draws below stay inside these ranges and needn't reach their ends.
Inputs may be any that keep to these rules, and one draw needn't show every extreme that they name: `lengths`: they sum to 16384; the longest is exactly 2048. `page_owner`: within the 64 entries of each index of seq, every owner appears exactly 2 times.
All inputs are finite; a program needn't handle non-finite values.
Results may differ from the reference program's by a relative error of at most 0.007.
The reference program's roundings to bfloat16 on the way (of `normed`, `probs` and `final`) count: a program that leaves them out, or rounds other values in their place, can miss the bound.
Values may be sent and summed in bfloat16 or wider, within the bound.
A program may use at most 192 MiB of HBM per device.

```python
import math
import jax
import jax.numpy as jnp
import numpy as np
from jax import lax

MODEL = 3584
DCAT = 7168
HEADS = 16
HEAD = 224
HH = 3584
RANK = 128
VOCAB = 32000
PAGE = 8
LOOKBACK = 4
NPROMPT = 12
REQ = 16
TOK_DEV = 512
TOKENS = 16384
MOST = 2048
PAGES_DEV = 64
PER_OWNER = 2
NPAGES = 2048
N_SEQ = 32


def draw_queries(key, part):
    base = jax.random.normal(jax.random.fold_in(key, 11), (TOKENS, HH), jnp.float32)
    return base.astype(jnp.bfloat16)


def draw_page_owner(key, part):
    blocks = jax.random.split(jax.random.fold_in(key, 21), N_SEQ)

    def one_device(block_key):
        return jax.random.permutation(block_key, PAGES_DEV) % N_SEQ
    return jax.vmap(one_device)(blocks).reshape(NPAGES).astype(jnp.int32)


def with_ends(array, own_key, smallest, largest):
    index_at = [jax.random.randint(jax.random.fold_in(own_key, axis), (), 0, length) for axis, length in enumerate(array.shape)]
    widest = array.shape.index(max(array.shape))
    beside = index_at[:widest] + [(index_at[widest] + 1) % array.shape[widest]] + index_at[widest + 1:]
    return array.at[tuple(index_at)].set(smallest).at[tuple(beside)].set(largest)


def block_scale(key, dims, cuts, low, high):
    level = 1.0
    for position, blocks in cuts:
        draws = jax.random.uniform(jax.random.fold_in(jax.random.fold_in(key, 6), position), (blocks,), jnp.float32, low / len(cuts), high / len(cuts))
        level = level * jnp.repeat(jnp.exp(draws), dims[position] // blocks).reshape((-1,) + (1,) * (len(dims) - 1 - position))
    return level


def split_up(count, total, most, slope):
    weights = [(1 << 20) // math.isqrt(rank ** slope) + 1 for rank in range(2, count + 1)]
    surplus, given = total - most - (count - 1), [1] * (count - 1)
    while surplus > 0:
        free = [i for i in range(count - 1) if given[i] < most]
        whole, remaining = sum([weights[i] for i in free]), surplus
        for i in free:
            more = min(most - given[i], max(1, remaining * weights[i] // whole), surplus)
            given[i] = given[i] + more
            surplus = surplus - more
    return np.array([most] + given)


def ragged(own_key, count, total, limit, slope):
    if count == 2:
        one = jax.random.randint(own_key, (), max(1, total - limit), min(limit, total - 1) + 1)
        return jnp.stack([one, total - one])
    sizes = jnp.asarray(split_up(count, total, limit, slope), jnp.int32)
    pairs = (count - 1) // 2
    donor, receiver = sizes[1:1 + 2 * pairs:2], sizes[2:2 + 2 * pairs:2]
    room = jnp.minimum(donor - 1, limit - receiver)
    moved = jax.random.randint(jax.random.fold_in(own_key, 1), (pairs,), 0, 1 << 20) % (room + 1)
    sizes = sizes.at[1:1 + 2 * pairs:2].set(donor - moved).at[2:2 + 2 * pairs:2].set(receiver + moved)
    return sizes[jax.random.permutation(jax.random.fold_in(own_key, 2), count)]


def noise(own_key, extent, scale, reach, cuts=(), held_as=jnp.bfloat16):
    result = jax.random.normal(own_key, extent, jnp.float32) * scale
    if len(cuts) > 0:
        result = block_scale(own_key, extent, cuts, -0.22, 0.18) * result
    return jnp.clip(result, min=-reach, max=reach).astype(held_as)


def setup_inputs(seed: int = 0) -> dict:
    streams_of = jax.random.split(jax.random.key(seed), 16)
    hidden_cat = noise(streams_of[0], (TOKENS, DCAT), 1.0, 6.0, ((0, 32),))
    norm_gain = jnp.clip(1.0 + 0.1 * jax.random.normal(streams_of[1], (DCAT,), jnp.float32), 0.5, 1.5)
    k_weight = noise(streams_of[2], (DCAT, HH), DCAT ** -0.5, 0.0625, ((0, 32), (1, 4)))
    v_weight = noise(streams_of[3], (DCAT, HH), DCAT ** -0.5, 0.0625, ((0, 32), (1, 4)))
    k_down = noise(streams_of[4], (DCAT, RANK), DCAT ** -0.5, 0.0625, ((0, 32),))
    v_down = noise(streams_of[5], (DCAT, RANK), DCAT ** -0.5, 0.0625, ((0, 32),))
    k_up = noise(streams_of[6], (RANK, HH), 0.04, 0.23925781, ((1, 4),))
    v_up = noise(streams_of[7], (RANK, HH), 0.04, 0.23925781, ((1, 4),))
    queries = draw_queries(jax.random.fold_in(streams_of[15], 71), 0)
    o_weight = noise(streams_of[9], (HH, MODEL), HH ** -0.5, 0.09375, ((0, 4),))
    final_gain = jnp.clip(1.0 + 0.1 * jax.random.normal(streams_of[10], (MODEL,), jnp.float32), 0.5, 1.5)
    unembed = noise(streams_of[11], (VOCAB, MODEL), 0.05, 0.29882812, ((0, 128),))
    lengths = ragged(streams_of[12], NPROMPT, TOKENS, MOST, 1).astype(jnp.int32)
    req_prompt = with_ends(jax.random.randint(streams_of[13], (REQ,), 0, NPROMPT), jax.random.fold_in(streams_of[13], 1), 0, NPROMPT - 1).astype(jnp.int32)
    page_owner = draw_page_owner(jax.random.fold_in(streams_of[15], 71), 0)
    return {"hidden_cat": hidden_cat, "norm_gain": norm_gain, "k_weight": k_weight, "v_weight": v_weight, "k_down": k_down, "v_down": v_down, "k_up": k_up, "v_up": v_up, "queries": queries, "o_weight": o_weight, "final_gain": final_gain, "unembed": unembed, "lengths": lengths, "req_prompt": req_prompt, "page_owner": page_owner}


def segment_of(positions, bounds):
    counted = lax.optimization_barrier(jnp.sum((bounds[None, :] <= positions[:, None]).astype(jnp.int32), axis=1))
    return jnp.where(positions < 0, -1, counted).astype(jnp.int32)

def project(normed, weight, down, up):
    base = jnp.dot(normed, weight, preferred_element_type=jnp.float32)
    low = jnp.dot(normed, down, preferred_element_type=jnp.float32).astype(jnp.bfloat16)
    return (base + jnp.dot(low, up, preferred_element_type=jnp.float32)).astype(jnp.bfloat16)

def reference(hidden_cat, norm_gain, k_weight, v_weight, k_down, v_down, k_up, v_up, queries, o_weight, final_gain, unembed, lengths, req_prompt, page_owner):
    wide = hidden_cat.astype(jnp.float32)
    inverse = lax.rsqrt(lax.optimization_barrier(jnp.mean(wide * wide, axis=1, keepdims=True)) + 1e-05)
    normed = (wide * inverse * norm_gain.astype(jnp.float32)).astype(jnp.bfloat16)
    key_rows = project(normed, k_weight, k_down, k_up)
    value_rows = project(normed, v_weight, v_down, v_up)
    bounds = jnp.cumsum(lengths).astype(jnp.int32)
    margin = LOOKBACK * TOK_DEV
    key_pad = jnp.concatenate([jnp.zeros((margin, HH), jnp.bfloat16), key_rows], axis=0)
    value_pad = jnp.concatenate([jnp.zeros((margin, HH), jnp.bfloat16), value_rows], axis=0)
    scale = 1.0 / HEAD ** 0.5

    def one_block(block_id):
        first_row = (block_id * TOK_DEV).astype(jnp.int32)
        query_pos = first_row + jnp.arange(TOK_DEV, dtype=jnp.int32)
        key_pos = first_row - margin + jnp.arange(margin + TOK_DEV, dtype=jnp.int32)
        query_block = lax.dynamic_slice_in_dim(queries, first_row, TOK_DEV, 0).astype(jnp.float32).reshape(TOK_DEV, HEADS, HEAD)
        key_block = lax.dynamic_slice_in_dim(key_pad, first_row, margin + TOK_DEV, 0).astype(jnp.float32).reshape(margin + TOK_DEV, HEADS, HEAD)
        value_block = lax.dynamic_slice_in_dim(value_pad, first_row, margin + TOK_DEV, 0).astype(jnp.float32).reshape(margin + TOK_DEV, HEADS, HEAD)
        scores = jnp.einsum('qhd,khd->hqk', query_block, key_block) * scale
        query_seg = segment_of(query_pos, bounds)
        key_seg = segment_of(key_pos, bounds)
        visible = (query_seg[:, None] == key_seg[None, :]) & (key_pos[None, :] <= query_pos[:, None])
        scores = jnp.where(visible[None], scores, -1e+30)
        row_max = lax.optimization_barrier(jnp.max(scores, axis=2, keepdims=True))
        expo_terms = jnp.exp(scores - row_max)
        probs = (expo_terms / lax.optimization_barrier(jnp.sum(expo_terms, axis=2, keepdims=True))).astype(jnp.bfloat16)
        mixed = jnp.einsum('hqk,khd->qhd', probs.astype(jnp.float32), value_block)
        return mixed.reshape(TOK_DEV, HH).astype(jnp.bfloat16)
    attended = lax.map(one_block, jnp.arange(TOKENS // TOK_DEV, dtype=jnp.int32)).reshape(TOKENS, HH)
    devices_n = NPAGES // PAGES_DEV
    owners = page_owner.reshape(devices_n, PAGES_DEV)
    onehot = (owners[:, :, None] == jnp.arange(devices_n, dtype=jnp.int32)[None, None, :]).astype(jnp.int32)
    before = jnp.cumsum(onehot, axis=1) - onehot
    earlier = lax.optimization_barrier(jnp.sum(before * onehot, axis=2))
    source = jnp.arange(devices_n, dtype=jnp.int32)[:, None]
    slots = (owners * PAGES_DEV + source * PER_OWNER + earlier).reshape(NPAGES).astype(jnp.int32)
    pages = jnp.stack([key_rows, value_rows], axis=1).reshape(NPAGES, PAGE, 2, HH)
    kv_cache = jnp.zeros_like(pages).at[slots].set(pages)
    last_pos = (bounds - 1)[req_prompt].astype(jnp.int32)
    rows = attended[last_pos]
    state = jnp.dot(rows, o_weight, preferred_element_type=jnp.float32)
    state_norm = jnp.sqrt(lax.optimization_barrier(jnp.sum(state * state, axis=1)))
    final = (state * lax.rsqrt(lax.optimization_barrier(jnp.mean(state * state, axis=1, keepdims=True)) + 1e-05) * final_gain).astype(jnp.bfloat16)
    logits = jnp.dot(final, unembed.T, preferred_element_type=jnp.float32)
    logit_max = lax.optimization_barrier(jnp.max(logits, axis=1))
    return (attended, kv_cache, state_norm, logit_max)
```

```python
import functools

import jax
import jax.numpy as jnp
from jax import lax
from jax.experimental import pallas as pl
from jax.experimental.pallas import tpu as pltpu
from jax.sharding import PartitionSpec as P

HEAD = 224
PAGE = 8
LOOKBACK = 4
NPROMPT = 12
RING = 4


def passed_along(value, axis, steps):
    count = lax.axis_size(axis)
    leading, last = (max(0, -steps), min(count, count - steps))
    return lax.ppermute(value, axis, [(source, source + steps) for source in range(leading, last)])


def segment_of(positions, bounds):
    counted = jnp.sum((bounds[None, :] <= positions[:, None]).astype(jnp.int32), axis=1)
    return jnp.where(positions < 0, -1, counted)


MESH = pl.DeviceIdType.MESH


def place(zs):
    s = lax.axis_index("seq")
    core = s % 2
    chip = s // 2
    return core, chip % zs, chip // zs


def seq_id(core, z, y, zs):
    return (y * zs + z) * 2 + core


def enter(peers):
    barrier = pltpu.get_barrier_semaphore()
    for peer in peers:
        pl.semaphore_signal(barrier, inc=1, device_id=peer, device_id_type=MESH)
    pl.semaphore_wait(barrier, len(peers))


def tail_kernel(
    zs,
    ys,
    tps,
    picked_ref,
    o_ref,
    gain_ref,
    un_ref,
    norm_ref,
    max_ref,
    o_buf,
    un_buf,
    row_c,
    row_z,
    row_y,
    sum_c,
    sum_z,
    parts,
    states,
    final_buf,
    max_own,
    max_got,
    send,
    recv,
    local_sem,
):
    core, z, y = place(zs)
    x = lax.axis_index("tp")
    rows, width = picked_ref.shape
    chunk = o_buf.shape[1]
    load_o = pltpu.make_async_copy(
        o_ref.at[:, pl.ds(pl.multiple_of(z * chunk, chunk), chunk)], o_buf, local_sem.at[0]
    )
    load_o.start()
    load_u = pltpu.make_async_copy(un_ref, un_buf, local_sem.at[1])
    load_u.start()
    on_core = [{"seq": seq_id(1 - core, z, y, zs)}]
    on_z = [{"seq": seq_id(core, (z + k) % zs, y, zs)} for k in range(1, zs)]
    on_y = [{"seq": seq_id(core, z, (y + k) % ys, zs)} for k in range(1, ys)]
    on_x = [{"tp": (x + k) % tps} for k in range(1, tps)]
    enter(on_core + on_z + on_y + on_x)
    used = [0]

    def exchange(peers, source, target):
        copies = []
        for k, peer in enumerate(peers):
            n = used[0]
            used[0] = n + 1
            copy = pltpu.make_async_remote_copy(
                src_ref=source,
                dst_ref=target(k),
                send_sem=send.at[n],
                recv_sem=recv.at[n],
                device_id=peer,
                device_id_type=MESH,
            )
            copy.start()
            copies.append(copy)
        return copies

    def finish(copies):
        for copy in copies:
            copy.wait()

    going = exchange(on_core, picked_ref, lambda k: row_c.at[k])
    final_buf[...] = jnp.zeros_like(final_buf)
    finish(going)
    sum_c[...] = picked_ref[...] + row_c[0]
    finish(exchange(on_z, sum_c, lambda k: row_z.at[k]))
    total = sum_c[...]
    for k in range(zs - 1):
        total = total + row_z[k]
    sum_z[...] = total
    finish(exchange(on_y, sum_z, lambda k: row_y.at[k]))
    for k in range(ys - 1):
        total = total + row_y[k]
    load_o.wait()
    parts[x] = jnp.dot(total, o_buf[...], preferred_element_type=jnp.float32)
    finish(exchange(on_x, parts.at[x], lambda k: parts.at[x]))
    state = parts[0]
    for k in range(1, tps):
        state = state + parts[k]
    states[z] = state
    finish(exchange(on_z, states.at[z], lambda k: states.at[z]))
    squares = jnp.zeros((rows, 1), jnp.float32)
    for k in range(zs):
        squares = squares + jnp.sum(states[k] * states[k], axis=1, keepdims=True)
    norm_ref[...] = jnp.broadcast_to(jnp.sqrt(squares), norm_ref.shape)
    inverse = lax.rsqrt(squares / (zs * chunk) + 1e-05)
    for k in range(zs):
        final_buf[k, 0:rows, :] = (
            states[k] * inverse * gain_ref[:, k * chunk : (k + 1) * chunk]
        ).astype(jnp.bfloat16)
    load_u.wait()
    logits = jnp.zeros((un_buf.shape[0], final_buf.shape[1]), jnp.float32)
    for k in range(zs):
        logits = logits + lax.dot_general(
            un_buf[:, k * chunk : (k + 1) * chunk],
            final_buf[k],
            (((1,), (1,)), ((), ())),
            preferred_element_type=jnp.float32,
        )
    best = jnp.broadcast_to(jnp.max(logits, axis=0, keepdims=True), max_ref.shape)
    place_at = 0
    for step, peers in enumerate((on_core, on_z, on_y, on_x)):
        max_own[step] = best
        start = place_at
        finish(exchange(peers, max_own.at[step], lambda k: max_got.at[start + k]))
        for k in range(len(peers)):
            best = jnp.maximum(best, max_got[start + k])
        place_at = place_at + len(peers)
    max_ref[...] = best


def tail(picked, o_weight, final_gain, unembed, zs, ys, tps):
    rows, width = picked.shape
    model = o_weight.shape[1]
    chunk = model // zs
    pads = 128
    copies = (1 + zs + ys + tps - 3) * 2 + zs - 1
    vmem = pl.BlockSpec(memory_space=pltpu.VMEM)
    anywhere = pl.BlockSpec(memory_space=pl.ANY)
    norm, best = pl.pallas_call(
        functools.partial(tail_kernel, zs, ys, tps),
        out_shape=(
            jax.ShapeDtypeStruct((rows, 128), jnp.float32),
            jax.ShapeDtypeStruct((8, pads), jnp.float32),
        ),
        in_specs=[vmem, anywhere, vmem, anywhere],
        out_specs=(vmem, vmem),
        scratch_shapes=[
            pltpu.VMEM((width, chunk), jnp.bfloat16),
            pltpu.VMEM(unembed.shape, jnp.bfloat16),
            pltpu.VMEM((1, rows, width), jnp.bfloat16),
            pltpu.VMEM((max(1, zs - 1), rows, width), jnp.bfloat16),
            pltpu.VMEM((max(1, ys - 1), rows, width), jnp.bfloat16),
            pltpu.VMEM((rows, width), jnp.bfloat16),
            pltpu.VMEM((rows, width), jnp.bfloat16),
            pltpu.VMEM((tps, rows, chunk), jnp.float32),
            pltpu.VMEM((zs, rows, chunk), jnp.float32),
            pltpu.VMEM((zs, pads, chunk), jnp.bfloat16),
            pltpu.VMEM((4, 8, pads), jnp.float32),
            pltpu.VMEM((1 + zs + ys + tps - 3, 8, pads), jnp.float32),
            pltpu.SemaphoreType.DMA((copies,)),
            pltpu.SemaphoreType.DMA((copies,)),
            pltpu.SemaphoreType.DMA((2,)),
        ],
        compiler_params=pltpu.CompilerParams(collective_id=0, has_side_effects=True),
        name="tail",
    )(picked, o_weight, final_gain.reshape(1, model), unembed)
    return norm[:, 0], best[0, :rows]


ORDER = (
    (0, 0),
    (1, 0),
    (3, 0),
    (0, 1),
    (0, 3),
    (2, 0),
    (1, 1),
    (1, 3),
    (3, 1),
    (3, 3),
    (0, 2),
    (2, 1),
    (2, 3),
    (1, 2),
    (3, 2),
    (2, 2),
)


def project_kernel(
    ring,
    hidden_ref,
    gain_ref,
    kw_ref,
    vw_ref,
    kd_ref,
    vd_ref,
    ku_ref,
    vu_ref,
    kv_ref,
    held,
    normed,
    total,
    send,
    recv,
    sib_send,
    sib_recv,
    local_sem,
):
    core, z, y = place(ring)
    rows = hidden_ref.shape[0]
    depth, width = kw_ref.shape
    rank = kd_ref.shape[1]
    half = depth // 2
    steps = len(ORDER)
    slot_of = {pair: n for n, pair in enumerate(ORDER)}

    def device(first, second):
        to_z = (z + first * (1 - core) + second * core + ring) % ring
        to_y = (y + first * core + second * (1 - core) + ring) % ring
        return {"seq": seq_id(core, to_z, to_y, ring)}

    sibling = {"seq": seq_id(1 - core, z, y, ring)}
    loads = []
    at = 0
    for n, ref in enumerate((kw_ref, vw_ref, kd_ref, vd_ref)):
        wide = ref.shape[1]
        load = pltpu.make_async_copy(ref, held.at[0, 0, :, at : at + wide], local_sem.at[n])
        load.start()
        loads.append(load)
        at = at + wide
    enter([device(1, 0), device(-1, 0), device(0, 1), device(0, -1), sibling])
    for load in loads:
        load.wait()

    plan = {}
    count = 0
    for slot, (i, j) in enumerate(ORDER):
        sends = []
        if (i, j) == (0, 0):
            sends += [((1, 0), (3, 0), 0), ((-1, 0), (1, 0), 0)]
        if j == 0:
            sends += [((0, 1), (i, 3), 0), ((0, -1), (i, 1), 0)]
        if (i, j) == (0, 0):
            sends += [((1, 0), (3, 0), 1), ((-1, 0), (1, 0), 1)]
        if (i, j) == (3, 0):
            sends += [((1, 0), (2, 0), 0)]
        if (i, j) == (1, 0):
            sends += [((-1, 0), (2, 0), 1)]
        if j == 0:
            sends += [((0, 1), (i, 3), 1), ((0, -1), (i, 1), 1)]
        if j == 3:
            sends += [((0, 1), (i, 2), 0)]
        if j == 1:
            sends += [((0, -1), (i, 2), 1)]
        plan[slot] = []
        for step, target, part in sends:
            plan[slot].append((step, slot_of[target], part, count))
            count = count + 1

    def piece(net, slot, part):
        return held.at[net, slot, pl.ds(part * half, half), :]

    def copy_out(slot, entry):
        step, target, part, n = entry
        return pltpu.make_async_remote_copy(
            src_ref=piece(0, slot, part),
            dst_ref=piece(0, target, part),
            send_sem=send.at[n],
            recv_sem=recv.at[target, part],
            device_id=device(*step),
            device_id_type=MESH,
        )

    def beside(slot):
        return pltpu.make_async_remote_copy(
            src_ref=held.at[0, slot],
            dst_ref=held.at[1, slot],
            send_sem=sib_send.at[slot],
            recv_sem=sib_recv.at[slot],
            device_id=sibling,
            device_id_type=MESH,
        )

    for entry in plan[0]:
        copy_out(0, entry).start()

    block = min(rows, 64)
    group = 4 * depth
    groups = hidden_ref.shape[1] // group

    @pl.loop(0, rows // block)
    def _(b):
        at_rows = pl.ds(pl.multiple_of(b * block, block), block)
        squares = jnp.zeros((block, 1), jnp.float32)
        for g in range(groups):
            wide = hidden_ref[at_rows, g * group : (g + 1) * group].astype(jnp.float32)
            squares = squares + jnp.sum(wide * wide, axis=1, keepdims=True)
        inverse = lax.rsqrt(squares / (groups * group) + 1e-05)
        for g in range(groups):
            wide = hidden_ref[at_rows, g * group : (g + 1) * group].astype(jnp.float32)
            scaled = wide * inverse * gain_ref[:, g * group : (g + 1) * group]
            for k in range(4):
                normed[g * 4 + k, at_rows, :] = scaled[:, k * depth : (k + 1) * depth].astype(
                    jnp.bfloat16
                )

    tile = min(512, total.shape[1])

    def add(net, slot, source):
        left = normed[source]
        for t in range(total.shape[1] // tile):
            cols = slice(t * tile, (t + 1) * tile)
            total[:, cols] += jnp.dot(
                left, held[net, slot, :, cols], preferred_element_type=jnp.float32
            )

    total[...] = jnp.zeros_like(total)

    @pl.loop(0, steps)
    def _(e):
        @pl.when(e > 0)
        def _():
            for part in range(2):
                pltpu.make_async_remote_copy(
                    src_ref=piece(0, e, part),
                    dst_ref=piece(0, e, part),
                    send_sem=send.at[0],
                    recv_sem=recv.at[e, part],
                    device_id=sibling,
                    device_id_type=MESH,
                ).wait_recv()

        for slot in range(1, steps):
            if plan[slot]:

                @pl.when(e == slot)
                def _(slot=slot):
                    for entry in plan[slot]:
                        copy_out(slot, entry).start()

        beside(e).start()
        first, second = 0, 0
        for slot, (i, j) in enumerate(ORDER):
            first = first + jnp.where(e == slot, i, 0)
            second = second + jnp.where(e == slot, j, 0)

        def source(kind):
            from_z = (z + first * (1 - kind) + second * kind) % ring
            from_y = (y + first * kind + second * (1 - kind)) % ring
            return seq_id(kind, from_z, from_y, ring)

        add(0, e, source(core))
        beside(e).wait_recv()
        add(1, e, source(1 - core))

    @pl.loop(0, rows // block)
    def _(b):
        at_rows = pl.ds(pl.multiple_of(b * block, block), block)
        for n, up in enumerate((ku_ref, vu_ref)):
            low = total[at_rows, 2 * width + n * rank : 2 * width + (n + 1) * rank]
            kv_ref[at_rows, n * width : (n + 1) * width] = (
                total[at_rows, n * width : (n + 1) * width]
                + jnp.dot(low.astype(jnp.bfloat16), up[...], preferred_element_type=jnp.float32)
            ).astype(jnp.bfloat16)

    for slot in range(steps):
        for entry in plan[slot]:
            copy_out(slot, entry).wait_send()
        beside(slot).wait_send()


def project(hidden_cat, norm_gain, k_weight, v_weight, k_down, v_down, k_up, v_up, ring):
    rows, wide = hidden_cat.shape
    depth, width = k_weight.shape
    rank = k_down.shape[1]
    columns = 2 * (width + rank)
    steps = ring * ring
    vmem = pl.BlockSpec(memory_space=pltpu.VMEM)
    anywhere = pl.BlockSpec(memory_space=pl.ANY)
    return pl.pallas_call(
        functools.partial(project_kernel, ring),
        out_shape=jax.ShapeDtypeStruct((rows, 2 * width), jnp.bfloat16),
        in_specs=[vmem, vmem, anywhere, anywhere, anywhere, anywhere, vmem, vmem],
        out_specs=vmem,
        scratch_shapes=[
            pltpu.VMEM((2, steps, depth, columns), jnp.bfloat16),
            pltpu.VMEM((2 * steps, rows, depth), jnp.bfloat16),
            pltpu.VMEM((rows, columns), jnp.float32),
            pltpu.SemaphoreType.DMA((32,)),
            pltpu.SemaphoreType.DMA((steps, 2)),
            pltpu.SemaphoreType.DMA((steps,)),
            pltpu.SemaphoreType.DMA((steps,)),
            pltpu.SemaphoreType.DMA((4,)),
        ],
        compiler_params=pltpu.CompilerParams(
            collective_id=1, has_side_effects=True, vmem_limit_bytes=62 << 20
        ),
        name="project",
    )(
        hidden_cat,
        norm_gain.reshape(1, wide),
        k_weight,
        v_weight,
        k_down,
        v_down,
        k_up,
        v_up,
    )


def local(
    hidden_cat,
    norm_gain,
    k_weight,
    v_weight,
    k_down,
    v_down,
    k_up,
    v_up,
    queries,
    o_weight,
    final_gain,
    unembed,
    lengths,
    req_prompt,
    page_owner,
):
    rows_here = hidden_cat.shape[0]
    width = k_weight.shape[1]
    heads_here = width // HEAD
    seq_count = lax.axis_size("seq")
    local_rows = project(
        hidden_cat, norm_gain, k_weight, v_weight, k_down, v_down, k_up, v_up, RING
    )
    local_kv = local_rows.reshape(rows_here, 2, width)
    kv_blocks = [local_kv]
    for offset in range(1, LOOKBACK + 1):
        kv_blocks.append(passed_along(local_kv, "seq", offset))
    bounds = jnp.cumsum(lengths)
    first_row = lax.axis_index("seq") * rows_here
    query_pos = first_row + jnp.arange(rows_here, dtype=jnp.int32)
    query_seg = segment_of(query_pos, bounds)
    query_heads = queries.reshape(rows_here, heads_here, HEAD)
    scale = 1.0 / HEAD**0.5
    score_list = []
    value_list = []
    for offset in range(LOOKBACK + 1):
        key_block = kv_blocks[offset][:, 0].reshape(rows_here, heads_here, HEAD)
        key_pos = query_pos - offset * rows_here
        key_seg = segment_of(key_pos, bounds)
        visible = (query_seg[:, None] == key_seg[None, :]) & (
            key_pos[None, :] <= query_pos[:, None]
        )

        def compute_scores(key_block=key_block, visible=visible):
            raw = (
                jnp.einsum(
                    "qhd,khd->hqk", query_heads, key_block, preferred_element_type=jnp.float32
                )
                * scale
            )
            return jnp.where(visible[None], raw, -1e30)

        blocked = compute_scores()
        score_list.append(blocked)
        value_list.append(kv_blocks[offset][:, 1].reshape(rows_here, heads_here, HEAD))
    scores = jnp.concatenate(score_list, axis=2)
    value_all = jnp.concatenate(value_list, axis=0)
    row_max = jnp.max(scores, axis=2, keepdims=True)
    expo_terms = jnp.exp(scores - row_max)
    probs = (expo_terms / jnp.sum(expo_terms, axis=2, keepdims=True)).astype(jnp.bfloat16)
    mixed = jnp.einsum("hqk,khd->qhd", probs, value_all, preferred_element_type=jnp.float32)
    attended = mixed.reshape(rows_here, width).astype(jnp.bfloat16)
    pages_here = rows_here // PAGE
    per_owner = pages_here // seq_count
    onehot = (page_owner[:, None] == jnp.arange(seq_count, dtype=jnp.int32)[None, :]).astype(
        jnp.int32
    )
    before = jnp.cumsum(onehot, axis=0) - onehot
    earlier = jnp.sum(before * onehot, axis=1)
    target = page_owner * per_owner + earlier
    pages = local_kv.reshape(pages_here, PAGE, 2, width)
    outgoing = jnp.zeros_like(pages).at[target].set(pages)
    kv_cache = lax.all_to_all(outgoing, "seq", split_axis=0, concat_axis=0, tiled=True)
    last_pos = bounds - 1
    request_pos = jnp.sum(
        jnp.where(
            req_prompt[:, None] == jnp.arange(NPROMPT, dtype=jnp.int32)[None, :],
            last_pos[None, :],
            0,
        ),
        axis=1,
    )
    selector = (request_pos[:, None] == query_pos[None, :]).astype(jnp.bfloat16)
    picked = jnp.dot(selector, attended, preferred_element_type=jnp.float32).astype(jnp.bfloat16)
    state_norm, logit_max = tail(
        picked, o_weight, final_gain, unembed, RING, RING, lax.axis_size("tp")
    )
    return (attended, kv_cache, state_norm, logit_max)


def solution(mesh):
    placed = (
        P("seq", None),
        P(),
        P("seq", "tp"),
        P("seq", "tp"),
        P("seq", None),
        P("seq", None),
        P(None, "tp"),
        P(None, "tp"),
        P("seq", "tp"),
        P("tp", None),
        P(),
        P(("seq", "tp"), None),
        P(),
        P(),
        P("seq"),
    )
    return jax.shard_map(
        local,
        mesh=mesh,
        in_specs=placed,
        out_specs=(P("seq", "tp"), P("seq", None, None, "tp"), P(), P()),
        check_vma=False,
    )
```

```python
import functools

import jax
import jax.numpy as jnp
from jax import lax
from jax.experimental import pallas as pl
from jax.experimental.pallas import tpu as pltpu
from jax.sharding import PartitionSpec as P

HEAD = 224
PAGE = 8
LOOKBACK = 4
NPROMPT = 12
RING = 4


MESH = pl.DeviceIdType.MESH


def place(zs):
    s = lax.axis_index("seq")
    core = s % 2
    chip = s // 2
    return core, chip % zs, chip // zs


def seq_id(core, z, y, zs):
    return (y * zs + z) * 2 + core


def enter(peers):
    barrier = pltpu.get_barrier_semaphore()
    for peer in peers:
        pl.semaphore_signal(barrier, inc=1, device_id=peer, device_id_type=MESH)
    pl.semaphore_wait(barrier, len(peers))


def tail_kernel(
    zs,
    ys,
    tps,
    picked_ref,
    o_ref,
    gain_ref,
    un_ref,
    norm_ref,
    max_ref,
    o_buf,
    un_buf,
    row_c,
    row_z,
    row_y,
    sum_c,
    sum_z,
    parts,
    states,
    final_buf,
    max_own,
    max_got,
    send,
    recv,
    local_sem,
):
    core, z, y = place(zs)
    x = lax.axis_index("tp")
    rows, width = picked_ref.shape
    chunk = o_buf.shape[1]
    load_o = pltpu.make_async_copy(
        o_ref.at[:, pl.ds(pl.multiple_of(z * chunk, chunk), chunk)], o_buf, local_sem.at[0]
    )
    load_o.start()
    load_u = pltpu.make_async_copy(un_ref, un_buf, local_sem.at[1])
    load_u.start()
    on_core = [{"seq": seq_id(1 - core, z, y, zs)}]
    on_z = [{"seq": seq_id(core, (z + k) % zs, y, zs)} for k in range(1, zs)]
    on_y = [{"seq": seq_id(core, z, (y + k) % ys, zs)} for k in range(1, ys)]
    on_x = [{"tp": (x + k) % tps} for k in range(1, tps)]
    enter(on_core + on_z + on_y + on_x)
    used = [0]

    def exchange(peers, source, target):
        copies = []
        for k, peer in enumerate(peers):
            n = used[0]
            used[0] = n + 1
            copy = pltpu.make_async_remote_copy(
                src_ref=source,
                dst_ref=target(k),
                send_sem=send.at[n],
                recv_sem=recv.at[n],
                device_id=peer,
                device_id_type=MESH,
            )
            copy.start()
            copies.append(copy)
        return copies

    def finish(copies):
        for copy in copies:
            copy.wait()

    going = exchange(on_core, picked_ref, lambda k: row_c.at[k])
    final_buf[...] = jnp.zeros_like(final_buf)
    finish(going)
    sum_c[...] = picked_ref[...] + row_c[0]
    finish(exchange(on_z, sum_c, lambda k: row_z.at[k]))
    total = sum_c[...]
    for k in range(zs - 1):
        total = total + row_z[k]
    sum_z[...] = total
    finish(exchange(on_y, sum_z, lambda k: row_y.at[k]))
    for k in range(ys - 1):
        total = total + row_y[k]
    load_o.wait()
    parts[x] = jnp.dot(total, o_buf[...], preferred_element_type=jnp.float32)
    finish(exchange(on_x, parts.at[x], lambda k: parts.at[x]))
    state = parts[0]
    for k in range(1, tps):
        state = state + parts[k]
    states[z] = state
    finish(exchange(on_z, states.at[z], lambda k: states.at[z]))
    squares = jnp.zeros((rows, 1), jnp.float32)
    for k in range(zs):
        squares = squares + jnp.sum(states[k] * states[k], axis=1, keepdims=True)
    norm_ref[...] = jnp.broadcast_to(jnp.sqrt(squares), norm_ref.shape)
    inverse = lax.rsqrt(squares / (zs * chunk) + 1e-05)
    for k in range(zs):
        final_buf[k, 0:rows, :] = (
            states[k] * inverse * gain_ref[:, k * chunk : (k + 1) * chunk]
        ).astype(jnp.bfloat16)
    load_u.wait()
    logits = jnp.zeros((un_buf.shape[0], final_buf.shape[1]), jnp.float32)
    for k in range(zs):
        logits = logits + lax.dot_general(
            un_buf[:, k * chunk : (k + 1) * chunk],
            final_buf[k],
            (((1,), (1,)), ((), ())),
            preferred_element_type=jnp.float32,
        )
    best = jnp.broadcast_to(jnp.max(logits, axis=0, keepdims=True), max_ref.shape)
    place_at = 0
    for step, peers in enumerate((on_core, on_z, on_y, on_x)):
        max_own[step] = best
        start = place_at
        finish(exchange(peers, max_own.at[step], lambda k: max_got.at[start + k]))
        for k in range(len(peers)):
            best = jnp.maximum(best, max_got[start + k])
        place_at = place_at + len(peers)
    max_ref[...] = best


def tail(picked, o_weight, final_gain, unembed, zs, ys, tps):
    rows, width = picked.shape
    model = o_weight.shape[1]
    chunk = model // zs
    pads = 128
    copies = (1 + zs + ys + tps - 3) * 2 + zs - 1
    vmem = pl.BlockSpec(memory_space=pltpu.VMEM)
    anywhere = pl.BlockSpec(memory_space=pl.ANY)
    norm, best = pl.pallas_call(
        functools.partial(tail_kernel, zs, ys, tps),
        out_shape=(
            jax.ShapeDtypeStruct((rows, 128), jnp.float32),
            jax.ShapeDtypeStruct((8, pads), jnp.float32),
        ),
        in_specs=[vmem, anywhere, vmem, anywhere],
        out_specs=(vmem, vmem),
        scratch_shapes=[
            pltpu.VMEM((width, chunk), jnp.bfloat16),
            pltpu.VMEM(unembed.shape, jnp.bfloat16),
            pltpu.VMEM((1, rows, width), jnp.bfloat16),
            pltpu.VMEM((max(1, zs - 1), rows, width), jnp.bfloat16),
            pltpu.VMEM((max(1, ys - 1), rows, width), jnp.bfloat16),
            pltpu.VMEM((rows, width), jnp.bfloat16),
            pltpu.VMEM((rows, width), jnp.bfloat16),
            pltpu.VMEM((tps, rows, chunk), jnp.float32),
            pltpu.VMEM((zs, rows, chunk), jnp.float32),
            pltpu.VMEM((zs, pads, chunk), jnp.bfloat16),
            pltpu.VMEM((4, 8, pads), jnp.float32),
            pltpu.VMEM((1 + zs + ys + tps - 3, 8, pads), jnp.float32),
            pltpu.SemaphoreType.DMA((copies,)),
            pltpu.SemaphoreType.DMA((copies,)),
            pltpu.SemaphoreType.DMA((2,)),
        ],
        compiler_params=pltpu.CompilerParams(collective_id=0, has_side_effects=True),
        name="tail",
    )(picked, o_weight, final_gain.reshape(1, model), unembed)
    return norm[:, 0], best[0, :rows]


ORDER = (
    (0, 0),
    (1, 0),
    (3, 0),
    (0, 1),
    (0, 3),
    (2, 0),
    (1, 1),
    (1, 3),
    (3, 1),
    (3, 3),
    (0, 2),
    (2, 1),
    (2, 3),
    (1, 2),
    (3, 2),
    (2, 2),
)


def project_kernel(
    ring,
    hidden_ref,
    gain_ref,
    kw_ref,
    vw_ref,
    kd_ref,
    vd_ref,
    ku_ref,
    vu_ref,
    kv_ref,
    held,
    normed,
    total,
    send,
    recv,
    sib_send,
    sib_recv,
    local_sem,
):
    core, z, y = place(ring)
    rows = hidden_ref.shape[0]
    depth, width = kw_ref.shape
    rank = kd_ref.shape[1]
    half = depth // 2
    steps = len(ORDER)
    slot_of = {pair: n for n, pair in enumerate(ORDER)}

    def device(first, second):
        to_z = (z + first * (1 - core) + second * core + ring) % ring
        to_y = (y + first * core + second * (1 - core) + ring) % ring
        return {"seq": seq_id(core, to_z, to_y, ring)}

    sibling = {"seq": seq_id(1 - core, z, y, ring)}
    loads = []
    at = 0
    for n, ref in enumerate((kw_ref, vw_ref, kd_ref, vd_ref)):
        wide = ref.shape[1]
        load = pltpu.make_async_copy(ref, held.at[0, 0, :, at : at + wide], local_sem.at[n])
        load.start()
        loads.append(load)
        at = at + wide
    enter([device(1, 0), device(-1, 0), device(0, 1), device(0, -1), sibling])
    for load in loads:
        load.wait()

    plan = {}
    count = 0
    for slot, (i, j) in enumerate(ORDER):
        sends = []
        if (i, j) == (0, 0):
            sends += [((1, 0), (3, 0), 0), ((-1, 0), (1, 0), 0)]
        if j == 0:
            sends += [((0, 1), (i, 3), 0), ((0, -1), (i, 1), 0)]
        if (i, j) == (0, 0):
            sends += [((1, 0), (3, 0), 1), ((-1, 0), (1, 0), 1)]
        if (i, j) == (3, 0):
            sends += [((1, 0), (2, 0), 0)]
        if (i, j) == (1, 0):
            sends += [((-1, 0), (2, 0), 1)]
        if j == 0:
            sends += [((0, 1), (i, 3), 1), ((0, -1), (i, 1), 1)]
        if j == 3:
            sends += [((0, 1), (i, 2), 0)]
        if j == 1:
            sends += [((0, -1), (i, 2), 1)]
        plan[slot] = []
        for step, target, part in sends:
            plan[slot].append((step, slot_of[target], part, count))
            count = count + 1

    def piece(net, slot, part):
        return held.at[net, slot, pl.ds(part * half, half), :]

    def copy_out(slot, entry):
        step, target, part, n = entry
        return pltpu.make_async_remote_copy(
            src_ref=piece(0, slot, part),
            dst_ref=piece(0, target, part),
            send_sem=send.at[n],
            recv_sem=recv.at[target, part],
            device_id=device(*step),
            device_id_type=MESH,
        )

    def beside(slot):
        return pltpu.make_async_remote_copy(
            src_ref=held.at[0, slot],
            dst_ref=held.at[1, slot],
            send_sem=sib_send.at[slot],
            recv_sem=sib_recv.at[slot],
            device_id=sibling,
            device_id_type=MESH,
        )

    for entry in plan[0]:
        copy_out(0, entry).start()

    block = min(rows, 64)
    group = 4 * depth
    groups = hidden_ref.shape[1] // group

    @pl.loop(0, rows // block)
    def _(b):
        at_rows = pl.ds(pl.multiple_of(b * block, block), block)
        squares = jnp.zeros((block, 1), jnp.float32)
        for g in range(groups):
            wide = hidden_ref[at_rows, g * group : (g + 1) * group].astype(jnp.float32)
            squares = squares + jnp.sum(wide * wide, axis=1, keepdims=True)
        inverse = lax.rsqrt(squares / (groups * group) + 1e-05)
        for g in range(groups):
            wide = hidden_ref[at_rows, g * group : (g + 1) * group].astype(jnp.float32)
            scaled = wide * inverse * gain_ref[:, g * group : (g + 1) * group]
            for k in range(4):
                normed[g * 4 + k, at_rows, :] = scaled[:, k * depth : (k + 1) * depth].astype(
                    jnp.bfloat16
                )

    tile = min(512, total.shape[1])

    def add(net, slot, source):
        left = normed[source]
        for t in range(total.shape[1] // tile):
            cols = slice(t * tile, (t + 1) * tile)
            total[:, cols] += jnp.dot(
                left, held[net, slot, :, cols], preferred_element_type=jnp.float32
            )

    total[...] = jnp.zeros_like(total)

    @pl.loop(0, steps)
    def _(e):
        @pl.when(e > 0)
        def _():
            for part in range(2):
                pltpu.make_async_remote_copy(
                    src_ref=piece(0, e, part),
                    dst_ref=piece(0, e, part),
                    send_sem=send.at[0],
                    recv_sem=recv.at[e, part],
                    device_id=sibling,
                    device_id_type=MESH,
                ).wait_recv()

        for slot in range(1, steps):
            if plan[slot]:

                @pl.when(e == slot)
                def _(slot=slot):
                    for entry in plan[slot]:
                        copy_out(slot, entry).start()

        beside(e).start()
        first, second = 0, 0
        for slot, (i, j) in enumerate(ORDER):
            first = first + jnp.where(e == slot, i, 0)
            second = second + jnp.where(e == slot, j, 0)

        def source(kind):
            from_z = (z + first * (1 - kind) + second * kind) % ring
            from_y = (y + first * kind + second * (1 - kind)) % ring
            return seq_id(kind, from_z, from_y, ring)

        add(0, e, source(core))
        beside(e).wait_recv()
        add(1, e, source(1 - core))

    @pl.loop(0, rows // block)
    def _(b):
        at_rows = pl.ds(pl.multiple_of(b * block, block), block)
        for n, up in enumerate((ku_ref, vu_ref)):
            low = total[at_rows, 2 * width + n * rank : 2 * width + (n + 1) * rank]
            kv_ref[at_rows, n * width : (n + 1) * width] = (
                total[at_rows, n * width : (n + 1) * width]
                + jnp.dot(low.astype(jnp.bfloat16), up[...], preferred_element_type=jnp.float32)
            ).astype(jnp.bfloat16)

    for slot in range(steps):
        for entry in plan[slot]:
            copy_out(slot, entry).wait_send()
        beside(slot).wait_send()


def project(hidden_cat, norm_gain, k_weight, v_weight, k_down, v_down, k_up, v_up, ring):
    rows, wide = hidden_cat.shape
    depth, width = k_weight.shape
    rank = k_down.shape[1]
    columns = 2 * (width + rank)
    steps = ring * ring
    vmem = pl.BlockSpec(memory_space=pltpu.VMEM)
    anywhere = pl.BlockSpec(memory_space=pl.ANY)
    return pl.pallas_call(
        functools.partial(project_kernel, ring),
        out_shape=jax.ShapeDtypeStruct((rows, 2 * width), jnp.bfloat16),
        in_specs=[vmem, vmem, anywhere, anywhere, anywhere, anywhere, vmem, vmem],
        out_specs=vmem,
        scratch_shapes=[
            pltpu.VMEM((2, steps, depth, columns), jnp.bfloat16),
            pltpu.VMEM((2 * steps, rows, depth), jnp.bfloat16),
            pltpu.VMEM((rows, columns), jnp.float32),
            pltpu.SemaphoreType.DMA((32,)),
            pltpu.SemaphoreType.DMA((steps, 2)),
            pltpu.SemaphoreType.DMA((steps,)),
            pltpu.SemaphoreType.DMA((steps,)),
            pltpu.SemaphoreType.DMA((4,)),
        ],
        compiler_params=pltpu.CompilerParams(
            collective_id=1, has_side_effects=True, vmem_limit_bytes=62 << 20
        ),
        name="project",
    )(
        hidden_cat,
        norm_gain.reshape(1, wide),
        k_weight,
        v_weight,
        k_down,
        v_down,
        k_up,
        v_up,
    )


def attend_kernel(
    ring,
    back,
    lengths_ref,
    request_ref,
    owner_ref,
    query_ref,
    kv_ref,
    out_ref,
    pages_ref,
    picked_ref,
    held,
    passing,
    outgoing,
    keys,
    values,
    query,
    mixed,
    top,
    weight,
    first_key,
    ahead_send,
    ahead_recv,
    back_send,
    back_recv,
    late_send,
    late_recv,
    sib_send,
    sib_recv,
    page_send,
    page_recv,
    local_sem,
):
    core, z, y = place(ring)
    chips = ring * ring
    chip = y * ring + z
    me = chip * 2 + core
    rows, double = kv_ref.shape
    width = double // 2
    heads = query.shape[0]
    size = width // heads
    load = pltpu.make_async_copy(kv_ref, held.at[0], local_sem.at[0])
    load.start()
    count = 2 * chips
    barrier = pltpu.get_barrier_semaphore()

    @pl.loop(1, count)
    def _(d):
        pl.semaphore_signal(
            barrier, inc=1, device_id={"seq": (me + d) % count}, device_id_type=MESH
        )

    pl.semaphore_wait(barrier, count - 1)
    load.wait()
    near = back[0][0]

    def remote(source, target, sent, got, device):
        return pltpu.make_async_remote_copy(
            src_ref=source,
            dst_ref=target,
            send_sem=sent,
            recv_sem=got,
            device_id={"seq": device},
            device_id_type=MESH,
        )

    next_chip = ((chip + 1) % chips) * 2 + core
    behind = (y * ring + (z + ring - 1) % ring) * 2 + core
    beyond = ((y * ring + (z + 1) % ring + 2) % chips) * 2 + core
    sibling = chip * 2 + 1 - core
    spans = ((0, near), (near, rows))

    def ahead(n):
        part = pl.ds(spans[n][0], spans[n][1] - spans[n][0])
        return remote(
            held.at[0, part], held.at[2, part], ahead_send.at[n], ahead_recv.at[n], next_chip
        )

    def backward(n):
        start, stop = back[n]
        return remote(
            held.at[0, pl.ds(start, stop - start)],
            passing.at[pl.ds(start - near, stop - start)],
            back_send.at[n],
            back_recv.at[n],
            behind,
        )

    def relay_ahead():
        part = pl.ds(0, near)
        return remote(
            held.at[2, part], held.at[4, part], late_send.at[0], late_recv.at[0], next_chip
        )

    def relay_back(n):
        start, stop = back[n]
        return remote(
            passing.at[pl.ds(start - near, stop - start)],
            held.at[4, pl.ds(start, stop - start)],
            late_send.at[1 + n],
            late_recv.at[1 + n],
            beyond,
        )

    def beside(n):
        return remote(
            held.at[2 * n + 2 * core],
            held.at[2 * n + 1],
            sib_send.at[n],
            sib_recv.at[n],
            sibling,
        )

    per = rows // count

    def page_copy(d):
        owner = (me + d) % count
        return remote(
            outgoing.at[pl.ds(pl.multiple_of(owner * per, per), per)],
            pages_ref.at[pl.ds(pl.multiple_of(me * per, per), per)],
            page_send.at[d],
            page_recv.at[d],
            owner,
        )

    for n in range(2):
        ahead(n).start()
    for n in range(len(back)):
        backward(n).start()

    @pl.when(core == 0)
    def _():
        beside(0).start()

    bounds = []
    running = 0
    for k in range(NPROMPT):
        running = running + lengths_ref[k]
        bounds.append(running)
    first_row = me * rows
    query_pos = first_row + lax.broadcasted_iota(jnp.int32, (rows, 1), 0)
    start_of = jnp.zeros((rows, 1), jnp.int32)
    for k in range(NPROMPT):
        start_of = jnp.where(query_pos >= bounds[k], bounds[k], start_of)
    first_key[...] = start_of
    for h in range(heads):
        query[h] = query_ref[:, h * size : (h + 1) * size]
    mixed[...] = jnp.zeros_like(mixed)
    top[...] = jnp.full_like(top, -1e30)
    weight[...] = jnp.zeros_like(weight)
    factor = 1.4426950408889634 / size**0.5
    tile = min(rows, 256)

    def order_pages():
        pages = owner_ref.shape[1]
        length = rows // pages
        square = (pages, pages)
        down = lax.broadcasted_iota(jnp.int32, square, 0)
        along = lax.broadcasted_iota(jnp.int32, square, 1)
        owner_row = jnp.broadcast_to(owner_ref[...], square).astype(jnp.float32)
        owner_col = jnp.sum(
            jnp.where(down == along, owner_row, 0.0), axis=1, keepdims=True
        )
        same = (owner_col == owner_row) & (down < along)
        earlier = jnp.sum(jnp.where(same, 1.0, 0.0), axis=0, keepdims=True)
        target = owner_row[0:1] * (pages // count) + earlier
        moves = jnp.where(down.astype(jnp.float32) == target, 1.0, 0.0).astype(jnp.bfloat16)
        spread = jnp.where(
            lax.broadcasted_iota(jnp.int32, (rows, pages), 0) // length
            == lax.broadcasted_iota(jnp.int32, (rows, pages), 1),
            1.0,
            0.0,
        ).astype(jnp.bfloat16)
        tall = jnp.dot(spread, moves, preferred_element_type=jnp.float32).astype(jnp.bfloat16)
        wide = lax.dot_general(
            tall, spread, (((1,), (1,)), ((), ())), preferred_element_type=jnp.float32
        )
        full = (rows, rows)
        aligned = (
            lax.broadcasted_iota(jnp.int32, full, 0) % length
            == lax.broadcasted_iota(jnp.int32, full, 1) % length
        )
        mover = jnp.where(aligned, wide, 0.0).astype(jnp.bfloat16)
        strip = min(256, double)
        for c in range(double // strip):
            cols = slice(c * strip, (c + 1) * strip)
            outgoing[:, cols] = jnp.dot(
                mover, held[0, :, cols], preferred_element_type=jnp.float32
            ).astype(jnp.bfloat16)

    @pl.loop(0, LOOKBACK + 1)
    def _(t):
        @pl.when(t == 1)
        def _():
            order_pages()
            ahead(0).wait_recv()
            relay_ahead().start()
            for n in range(len(back)):
                backward(n).wait_recv()
                relay_back(n).start()

            @pl.loop(1, count)
            def _(d):
                page_copy(d).start()

            mine = pl.ds(pl.multiple_of(me * per, per), per)
            pltpu.make_async_copy(outgoing.at[mine], pages_ref.at[mine], local_sem.at[1]).start()
            ahead(1).wait_recv()

            @pl.when(core == 1)
            def _():
                beside(0).start()

            @pl.when(core == 0)
            def _():
                beside(1).start()

        @pl.when(t == 2)
        def _():
            beside(0).wait_recv()

        @pl.when(t == 3)
        def _():
            relay_ahead().wait_recv()
            for n in range(len(back)):
                relay_back(n).wait_recv()

            @pl.when(core == 1)
            def _():
                beside(1).start()

        @pl.when(t == 4)
        def _():
            beside(1).wait_recv()

        offset = 0
        for n, value in enumerate((0, 2, 1, 4, 3)):
            offset = offset + jnp.where(t == n, value, 0)
        key_pos = (me - offset) * rows + lax.broadcasted_iota(jnp.int32, (1, rows), 1)
        for h in range(heads):
            keys[...] = held[offset, :, h * size : (h + 1) * size]
            values[...] = held[offset, :, width + h * size : width + (h + 1) * size]

            @pl.loop(0, rows // tile)
            def _(b, h=h):
                part = pl.ds(pl.multiple_of(b * tile, tile), tile)
                raw = lax.dot_general(
                    query[h, part, :],
                    keys[...],
                    (((1,), (1,)), ((), ())),
                    preferred_element_type=jnp.float32,
                )
                here = first_row + b * tile + lax.broadcasted_iota(jnp.int32, (tile, 1), 0)
                visible = (key_pos >= first_key[part, :]) & (key_pos <= here)
                scores = jnp.where(visible, raw * factor, -1e30)
                old = top[h, part, :]
                new = jnp.maximum(old, jnp.max(scores, axis=1, keepdims=True))
                terms = jnp.exp2(scores - new)
                shrink = jnp.exp2(old - new)
                weight[h, part, :] = weight[h, part, :] * shrink + jnp.sum(
                    terms, axis=1, keepdims=True
                )
                mixed[h, part, :] = mixed[h, part, :] * shrink + jnp.dot(
                    terms.astype(jnp.bfloat16), values[...], preferred_element_type=jnp.float32
                )
                top[h, part, :] = new

    for h in range(heads):
        out_ref[:, h * size : (h + 1) * size] = (mixed[h] / weight[h]).astype(jnp.bfloat16)
    requests = picked_ref.shape[0]
    which = lax.broadcasted_iota(jnp.int32, (requests, 1), 0)
    last = jnp.zeros((requests, 1), jnp.int32)
    for r in range(requests):
        end = 0
        for k in range(NPROMPT):
            end = end + jnp.where(request_ref[r] == k, bounds[k], 0)
        last = jnp.where(which == r, end - 1, last)
    chosen = jnp.where(
        last == first_row + lax.broadcasted_iota(jnp.int32, (requests, rows), 1), 1.0, 0.0
    ).astype(jnp.bfloat16)
    picked_ref[...] = jnp.dot(
        chosen, out_ref[...], preferred_element_type=jnp.float32
    ).astype(jnp.bfloat16)

    for n in range(2):
        ahead(n).wait_send()
        beside(n).wait_send()
    relay_ahead().wait_send()
    for n in range(len(back)):
        backward(n).wait_send()
        relay_back(n).wait_send()

    @pl.loop(1, count)
    def _(d):
        page_copy(d).wait()

    mine = pl.ds(pl.multiple_of(me * per, per), per)
    pltpu.make_async_copy(outgoing.at[mine], pages_ref.at[mine], local_sem.at[1]).wait()


def attend(lengths, req_prompt, page_owner, queries, local_rows, ring):
    rows, width = queries.shape
    heads = width // HEAD
    count = 2 * ring * ring
    near = rows * 11 // 32
    third = (rows - near) // 3
    back = tuple((near + n * third, near + (n + 1) * third) for n in range(3))
    vmem = pl.BlockSpec(memory_space=pltpu.VMEM)
    smem = pl.BlockSpec(memory_space=pltpu.SMEM)
    anywhere = pl.BlockSpec(memory_space=pl.ANY)
    dma = pltpu.SemaphoreType.DMA
    return pl.pallas_call(
        functools.partial(attend_kernel, ring, back),
        out_shape=(
            jax.ShapeDtypeStruct((rows, width), jnp.bfloat16),
            jax.ShapeDtypeStruct((rows, 2 * width), jnp.bfloat16),
            jax.ShapeDtypeStruct((req_prompt.shape[0], width), jnp.bfloat16),
        ),
        in_specs=[smem, smem, vmem, vmem, anywhere],
        out_specs=(vmem, anywhere, vmem),
        scratch_shapes=[
            pltpu.VMEM((LOOKBACK + 1, rows, 2 * width), jnp.bfloat16),
            pltpu.VMEM((rows - near, 2 * width), jnp.bfloat16),
            pltpu.VMEM((rows, 2 * width), jnp.bfloat16),
            pltpu.VMEM((rows, HEAD), jnp.bfloat16),
            pltpu.VMEM((rows, HEAD), jnp.bfloat16),
            pltpu.VMEM((heads, rows, HEAD), jnp.bfloat16),
            pltpu.VMEM((heads, rows, HEAD), jnp.float32),
            pltpu.VMEM((heads, rows, 1), jnp.float32),
            pltpu.VMEM((heads, rows, 1), jnp.float32),
            pltpu.VMEM((rows, 1), jnp.int32),
            dma((2,)),
            dma((2,)),
            dma((3,)),
            dma((3,)),
            dma((4,)),
            dma((4,)),
            dma((2,)),
            dma((2,)),
            dma((count,)),
            dma((count,)),
            dma((2,)),
        ],
        compiler_params=pltpu.CompilerParams(
            collective_id=2, has_side_effects=True, vmem_limit_bytes=60 << 20
        ),
        name="attend",
    )(lengths, req_prompt, page_owner.reshape(1, -1), queries, local_rows)


def local(
    hidden_cat,
    norm_gain,
    k_weight,
    v_weight,
    k_down,
    v_down,
    k_up,
    v_up,
    queries,
    o_weight,
    final_gain,
    unembed,
    lengths,
    req_prompt,
    page_owner,
):
    local_rows = project(
        hidden_cat, norm_gain, k_weight, v_weight, k_down, v_down, k_up, v_up, RING
    )
    attended, pages, picked = attend(lengths, req_prompt, page_owner, queries, local_rows, RING)
    rows, width = attended.shape
    kv_cache = pages.reshape(rows // PAGE, PAGE, 2, width)
    state_norm, logit_max = tail(
        picked, o_weight, final_gain, unembed, RING, RING, lax.axis_size("tp")
    )
    return (attended, kv_cache, state_norm, logit_max)


def solution(mesh):
    placed = (
        P("seq", None),
        P(),
        P("seq", "tp"),
        P("seq", "tp"),
        P("seq", None),
        P("seq", None),
        P(None, "tp"),
        P(None, "tp"),
        P("seq", "tp"),
        P("tp", None),
        P(),
        P(("seq", "tp"), None),
        P(),
        P(),
        P("seq"),
    )
    return jax.shard_map(
        local,
        mesh=mesh,
        in_specs=placed,
        out_specs=(P("seq", "tp"), P("seq", None, None, "tp"), P(), P()),
        check_vma=False,
    )
```

```python
import functools

import jax
import jax.numpy as jnp
from jax import lax
from jax.experimental import pallas as pl
from jax.experimental.pallas import tpu as pltpu
from jax.sharding import PartitionSpec as P

HEAD = 224
PAGE = 8
LOOKBACK = 4
NPROMPT = 12
RING = 4


MESH = pl.DeviceIdType.MESH


def place(zs):
    s = lax.axis_index("seq")
    core = s % 2
    chip = s // 2
    return core, chip % zs, chip // zs


def seq_id(core, z, y, zs):
    return (y * zs + z) * 2 + core


def enter(peers):
    barrier = pltpu.get_barrier_semaphore()
    for peer in peers:
        pl.semaphore_signal(barrier, inc=1, device_id=peer, device_id_type=MESH)
    pl.semaphore_wait(barrier, len(peers))


def last_tokens(
    ring,
    tps,
    fill,
    picked,
    o_buf,
    gain_ref,
    un_buf,
    norm_ref,
    max_ref,
    row_a,
    row_b,
    row_sum,
    parts,
    states,
    final_buf,
    max_own,
    max_got,
    send,
    recv,
    load_o,
    load_u,
):
    core, z, y = place(ring)
    x = lax.axis_index("tp")
    rows, width = picked.shape
    chunk = o_buf.shape[1]
    near = [
        {"seq": seq_id((core + c) % 2, (z + k) % ring, y, ring)}
        for k in range(ring)
        for c in range(2)
        if k + c > 0
    ]
    on_z = [{"seq": seq_id(core, (z + k) % ring, y, ring)} for k in range(1, ring)]
    on_y = [{"seq": seq_id(core, z, (y + k) % ring, ring)} for k in range(1, ring)]
    on_x = [{"tp": (x + k) % tps} for k in range(1, tps)]
    far = [
        {"seq": seq_id(core, z, (y + k) % ring, ring), "tp": (x + j) % tps}
        for k in range(ring)
        for j in range(tps)
        if k + j > 0
    ]
    used = [0]

    def exchange(peers, source, target):
        copies = []
        for k, peer in enumerate(peers):
            n = used[0]
            used[0] = n + 1
            copy = pltpu.make_async_remote_copy(
                src_ref=source,
                dst_ref=target(k),
                send_sem=send.at[n],
                recv_sem=recv.at[n],
                device_id=peer,
                device_id_type=MESH,
            )
            copy.start()
            copies.append(copy)
        fill()
        for copy in copies:
            copy.wait()

    exchange(near, picked, lambda k: row_a.at[k])
    total = picked[...]
    for k in range(len(near)):
        total = total + row_a[k]
    row_sum[...] = total
    exchange(on_y, row_sum, lambda k: row_b.at[k])
    for k in range(len(on_y)):
        total = total + row_b[k]
    load_o.wait()
    parts[x] = jnp.dot(total, o_buf[...], preferred_element_type=jnp.float32)
    exchange(on_x, parts.at[x], lambda k: parts.at[x])
    state = parts[0]
    for k in range(1, tps):
        state = state + parts[k]
    states[z] = state
    exchange(on_z, states.at[z], lambda k: states.at[z])
    squares = jnp.zeros((rows, 1), jnp.float32)
    for k in range(ring):
        squares = squares + jnp.sum(states[k] * states[k], axis=1, keepdims=True)
    norm_ref[...] = jnp.broadcast_to(jnp.sqrt(squares), norm_ref.shape)
    inverse = lax.rsqrt(squares / (ring * chunk) + 1e-05)
    for k in range(ring):
        final_buf[k, 0:rows, :] = (
            states[k] * inverse * gain_ref[:, k * chunk : (k + 1) * chunk]
        ).astype(jnp.bfloat16)
    load_u.wait()
    logits = jnp.zeros((un_buf.shape[0], final_buf.shape[1]), jnp.float32)
    for k in range(ring):
        logits = logits + lax.dot_general(
            un_buf[:, k * chunk : (k + 1) * chunk],
            final_buf[k],
            (((1,), (1,)), ((), ())),
            preferred_element_type=jnp.float32,
        )
    best = jnp.broadcast_to(jnp.max(logits, axis=0, keepdims=True), max_ref.shape)
    start = 0
    for step, peers in enumerate((near, far)):
        max_own[step] = best
        exchange(peers, max_own.at[step], lambda k, start=start: max_got.at[start + k])
        for k in range(len(peers)):
            best = jnp.maximum(best, max_got[start + k])
        start = start + len(peers)
    max_ref[...] = best


ORDER = (
    (0, 0),
    (1, 0),
    (3, 0),
    (0, 1),
    (0, 3),
    (2, 0),
    (1, 1),
    (1, 3),
    (3, 1),
    (3, 3),
    (0, 2),
    (2, 1),
    (2, 3),
    (1, 2),
    (3, 2),
    (2, 2),
)


def project_kernel(
    ring,
    hidden_ref,
    gain_ref,
    kw_ref,
    vw_ref,
    kd_ref,
    vd_ref,
    ku_ref,
    vu_ref,
    kv_ref,
    held,
    normed,
    total,
    send,
    recv,
    sib_send,
    sib_recv,
    local_sem,
):
    core, z, y = place(ring)
    rows = hidden_ref.shape[0]
    depth, width = kw_ref.shape
    rank = kd_ref.shape[1]
    half = depth // 2
    steps = len(ORDER)
    slot_of = {pair: n for n, pair in enumerate(ORDER)}

    def device(first, second):
        to_z = (z + first * (1 - core) + second * core + ring) % ring
        to_y = (y + first * core + second * (1 - core) + ring) % ring
        return {"seq": seq_id(core, to_z, to_y, ring)}

    sibling = {"seq": seq_id(1 - core, z, y, ring)}
    loads = []
    at = 0
    for n, ref in enumerate((kw_ref, vw_ref, kd_ref, vd_ref)):
        wide = ref.shape[1]
        load = pltpu.make_async_copy(ref, held.at[0, 0, :, at : at + wide], local_sem.at[n])
        load.start()
        loads.append(load)
        at = at + wide
    enter([device(1, 0), device(-1, 0), device(0, 1), device(0, -1), sibling])
    for load in loads:
        load.wait()

    plan = {}
    count = 0
    for slot, (i, j) in enumerate(ORDER):
        sends = []
        if (i, j) == (0, 0):
            sends += [((1, 0), (3, 0), 0), ((-1, 0), (1, 0), 0)]
        if j == 0:
            sends += [((0, 1), (i, 3), 0), ((0, -1), (i, 1), 0)]
        if (i, j) == (0, 0):
            sends += [((1, 0), (3, 0), 1), ((-1, 0), (1, 0), 1)]
        if (i, j) == (3, 0):
            sends += [((1, 0), (2, 0), 0)]
        if (i, j) == (1, 0):
            sends += [((-1, 0), (2, 0), 1)]
        if j == 0:
            sends += [((0, 1), (i, 3), 1), ((0, -1), (i, 1), 1)]
        if j == 3:
            sends += [((0, 1), (i, 2), 0)]
        if j == 1:
            sends += [((0, -1), (i, 2), 1)]
        plan[slot] = []
        for step, target, part in sends:
            plan[slot].append((step, slot_of[target], part, count))
            count = count + 1

    def piece(net, slot, part):
        return held.at[net, slot, pl.ds(part * half, half), :]

    def copy_out(slot, entry):
        step, target, part, n = entry
        return pltpu.make_async_remote_copy(
            src_ref=piece(0, slot, part),
            dst_ref=piece(0, target, part),
            send_sem=send.at[n],
            recv_sem=recv.at[target, part],
            device_id=device(*step),
            device_id_type=MESH,
        )

    def beside(slot):
        return pltpu.make_async_remote_copy(
            src_ref=held.at[0, slot],
            dst_ref=held.at[1, slot],
            send_sem=sib_send.at[slot],
            recv_sem=sib_recv.at[slot],
            device_id=sibling,
            device_id_type=MESH,
        )

    for entry in plan[0]:
        copy_out(0, entry).start()

    block = min(rows, 64)
    group = 4 * depth
    groups = hidden_ref.shape[1] // group

    @pl.loop(0, rows // block)
    def _(b):
        at_rows = pl.ds(pl.multiple_of(b * block, block), block)
        squares = jnp.zeros((block, 1), jnp.float32)
        for g in range(groups):
            wide = hidden_ref[at_rows, g * group : (g + 1) * group].astype(jnp.float32)
            squares = squares + jnp.sum(wide * wide, axis=1, keepdims=True)
        inverse = lax.rsqrt(squares / (groups * group) + 1e-05)
        for g in range(groups):
            wide = hidden_ref[at_rows, g * group : (g + 1) * group].astype(jnp.float32)
            scaled = wide * inverse * gain_ref[:, g * group : (g + 1) * group]
            for k in range(4):
                normed[g * 4 + k, at_rows, :] = scaled[:, k * depth : (k + 1) * depth].astype(
                    jnp.bfloat16
                )

    tile = min(512, total.shape[1])

    def add(net, slot, source):
        left = normed[source]
        for t in range(total.shape[1] // tile):
            cols = slice(t * tile, (t + 1) * tile)
            total[:, cols] += jnp.dot(
                left, held[net, slot, :, cols], preferred_element_type=jnp.float32
            )

    total[...] = jnp.zeros_like(total)

    @pl.loop(0, steps)
    def _(e):
        @pl.when(e > 0)
        def _():
            for part in range(2):
                pltpu.make_async_remote_copy(
                    src_ref=piece(0, e, part),
                    dst_ref=piece(0, e, part),
                    send_sem=send.at[0],
                    recv_sem=recv.at[e, part],
                    device_id=sibling,
                    device_id_type=MESH,
                ).wait_recv()

        for slot in range(1, steps):
            if plan[slot]:

                @pl.when(e == slot)
                def _(slot=slot):
                    for entry in plan[slot]:
                        copy_out(slot, entry).start()

        beside(e).start()
        first, second = 0, 0
        for slot, (i, j) in enumerate(ORDER):
            first = first + jnp.where(e == slot, i, 0)
            second = second + jnp.where(e == slot, j, 0)

        def source(kind):
            from_z = (z + first * (1 - kind) + second * kind) % ring
            from_y = (y + first * kind + second * (1 - kind)) % ring
            return seq_id(kind, from_z, from_y, ring)

        add(0, e, source(core))
        beside(e).wait_recv()
        add(1, e, source(1 - core))

    @pl.loop(0, rows // block)
    def _(b):
        at_rows = pl.ds(pl.multiple_of(b * block, block), block)
        for n, up in enumerate((ku_ref, vu_ref)):
            low = total[at_rows, 2 * width + n * rank : 2 * width + (n + 1) * rank]
            kv_ref[at_rows, n * width : (n + 1) * width] = (
                total[at_rows, n * width : (n + 1) * width]
                + jnp.dot(low.astype(jnp.bfloat16), up[...], preferred_element_type=jnp.float32)
            ).astype(jnp.bfloat16)

    for slot in range(steps):
        for entry in plan[slot]:
            copy_out(slot, entry).wait_send()
        beside(slot).wait_send()


def project(hidden_cat, norm_gain, k_weight, v_weight, k_down, v_down, k_up, v_up, ring):
    rows, wide = hidden_cat.shape
    depth, width = k_weight.shape
    rank = k_down.shape[1]
    columns = 2 * (width + rank)
    steps = ring * ring
    vmem = pl.BlockSpec(memory_space=pltpu.VMEM)
    anywhere = pl.BlockSpec(memory_space=pl.ANY)
    return pl.pallas_call(
        functools.partial(project_kernel, ring),
        out_shape=jax.ShapeDtypeStruct((rows, 2 * width), jnp.bfloat16),
        in_specs=[vmem, vmem, anywhere, anywhere, anywhere, anywhere, vmem, vmem],
        out_specs=vmem,
        scratch_shapes=[
            pltpu.VMEM((2, steps, depth, columns), jnp.bfloat16),
            pltpu.VMEM((2 * steps, rows, depth), jnp.bfloat16),
            pltpu.VMEM((rows, columns), jnp.float32),
            pltpu.SemaphoreType.DMA((32,)),
            pltpu.SemaphoreType.DMA((steps, 2)),
            pltpu.SemaphoreType.DMA((steps,)),
            pltpu.SemaphoreType.DMA((steps,)),
            pltpu.SemaphoreType.DMA((4,)),
        ],
        compiler_params=pltpu.CompilerParams(
            collective_id=1, has_side_effects=True, vmem_limit_bytes=62 << 20
        ),
        name="project",
    )(
        hidden_cat,
        norm_gain.reshape(1, wide),
        k_weight,
        v_weight,
        k_down,
        v_down,
        k_up,
        v_up,
    )


def attend_kernel(
    ring,
    tps,
    back,
    lengths_ref,
    request_ref,
    owner_ref,
    query_ref,
    kv_ref,
    o_ref,
    gain_ref,
    un_ref,
    out_ref,
    pages_ref,
    norm_ref,
    max_ref,
    held,
    passing,
    outgoing,
    keys,
    values,
    query,
    mixed,
    top,
    weight,
    first_key,
    ahead_send,
    ahead_recv,
    back_send,
    back_recv,
    late_send,
    late_recv,
    sib_send,
    sib_recv,
    page_send,
    page_recv,
    local_sem,
    picked_ref,
    o_buf,
    un_buf,
    row_a,
    row_b,
    row_sum,
    parts,
    states,
    final_buf,
    max_own,
    max_got,
    tail_send,
    tail_recv,
):
    core, z, y = place(ring)
    chips = ring * ring
    chip = y * ring + z
    me = chip * 2 + core
    rows, double = kv_ref.shape
    width = double // 2
    heads = query.shape[0]
    size = width // heads
    load = pltpu.make_async_copy(kv_ref, held.at[0], local_sem.at[0])
    load.start()
    chunk = o_buf.shape[1]
    load_o = pltpu.make_async_copy(
        o_ref.at[:, pl.ds(pl.multiple_of(z * chunk, chunk), chunk)], o_buf, local_sem.at[2]
    )
    load_o.start()
    load_u = pltpu.make_async_copy(un_ref, un_buf, local_sem.at[3])
    load_u.start()
    count = 2 * chips
    x = lax.axis_index("tp")
    barrier = pltpu.get_barrier_semaphore()

    @pl.loop(1, count)
    def _(d):
        pl.semaphore_signal(
            barrier, inc=1, device_id={"seq": (me + d) % count}, device_id_type=MESH
        )

    for k in range(ring):
        for j in range(1, tps):
            pl.semaphore_signal(
                barrier,
                inc=1,
                device_id={"seq": seq_id(core, z, (y + k) % ring, ring), "tp": (x + j) % tps},
                device_id_type=MESH,
            )
    pl.semaphore_wait(barrier, count - 1 + ring * (tps - 1))
    load.wait()
    near = back[0][0]

    def remote(source, target, sent, got, device):
        return pltpu.make_async_remote_copy(
            src_ref=source,
            dst_ref=target,
            send_sem=sent,
            recv_sem=got,
            device_id={"seq": device},
            device_id_type=MESH,
        )

    next_chip = ((chip + 1) % chips) * 2 + core
    behind = (y * ring + (z + ring - 1) % ring) * 2 + core
    beyond = ((y * ring + (z + 1) % ring + 2) % chips) * 2 + core
    sibling = chip * 2 + 1 - core
    spans = ((0, near), (near, rows))

    def ahead(n):
        part = pl.ds(spans[n][0], spans[n][1] - spans[n][0])
        return remote(
            held.at[0, part], held.at[2, part], ahead_send.at[n], ahead_recv.at[n], next_chip
        )

    def backward(n):
        start, stop = back[n]
        return remote(
            held.at[0, pl.ds(start, stop - start)],
            passing.at[pl.ds(start - near, stop - start)],
            back_send.at[n],
            back_recv.at[n],
            behind,
        )

    def relay_ahead():
        part = pl.ds(0, near)
        return remote(
            held.at[2, part], held.at[4, part], late_send.at[0], late_recv.at[0], next_chip
        )

    def relay_back(n):
        start, stop = back[n]
        return remote(
            passing.at[pl.ds(start - near, stop - start)],
            held.at[4, pl.ds(start, stop - start)],
            late_send.at[1 + n],
            late_recv.at[1 + n],
            beyond,
        )

    def beside(n):
        return remote(
            held.at[2 * n + 2 * core],
            held.at[2 * n + 1],
            sib_send.at[n],
            sib_recv.at[n],
            sibling,
        )

    per = rows // count

    def page_copy(d):
        down, along, other = d
        owner = seq_id((core + other) % 2, (z + along) % ring, (y + down) % ring, ring)
        n = (down * ring + along) * 2 + other
        return remote(
            outgoing.at[pl.ds(pl.multiple_of(owner * per, per), per)],
            pages_ref.at[pl.ds(pl.multiple_of(me * per, per), per)],
            page_send.at[n],
            page_recv.at[n],
            owner,
        )

    flat = [(k, 0, c) for k in range(ring) for c in range(2) if k + c > 0]
    batches = [
        [(k, 1, 0), ((ring - k) % ring, ring - 1, 0), (k, 1, 1), ((ring - k) % ring, ring - 1, 1)]
        for k in range(ring)
    ] + [[(k, 2, 0), (k, 2, 1), (k + 2, 2, 0), (k + 2, 2, 1)] for k in range(2)]
    waiting = list(batches)

    def fill():
        if waiting:
            for d in waiting.pop(0):
                page_copy(d).start()

    for n in range(2):
        ahead(n).start()
    for n in range(len(back)):
        backward(n).start()

    @pl.when(core == 0)
    def _():
        beside(0).start()

    bounds = []
    running = 0
    for k in range(NPROMPT):
        running = running + lengths_ref[k]
        bounds.append(running)
    first_row = me * rows
    query_pos = first_row + lax.broadcasted_iota(jnp.int32, (rows, 1), 0)
    start_of = jnp.zeros((rows, 1), jnp.int32)
    for k in range(NPROMPT):
        start_of = jnp.where(query_pos >= bounds[k], bounds[k], start_of)
    first_key[...] = start_of
    for h in range(heads):
        query[h] = query_ref[:, h * size : (h + 1) * size]
    mixed[...] = jnp.zeros_like(mixed)
    top[...] = jnp.full_like(top, -1e30)
    weight[...] = jnp.zeros_like(weight)
    factor = 1.4426950408889634 / size**0.5
    tile = min(rows, 256)

    def order_pages():
        pages = owner_ref.shape[1]
        length = rows // pages
        square = (pages, pages)
        down = lax.broadcasted_iota(jnp.int32, square, 0)
        along = lax.broadcasted_iota(jnp.int32, square, 1)
        owner_row = jnp.broadcast_to(owner_ref[...], square).astype(jnp.float32)
        owner_col = jnp.sum(
            jnp.where(down == along, owner_row, 0.0), axis=1, keepdims=True
        )
        same = (owner_col == owner_row) & (down < along)
        earlier = jnp.sum(jnp.where(same, 1.0, 0.0), axis=0, keepdims=True)
        target = owner_row[0:1] * (pages // count) + earlier
        moves = jnp.where(down.astype(jnp.float32) == target, 1.0, 0.0).astype(jnp.bfloat16)
        spread = jnp.where(
            lax.broadcasted_iota(jnp.int32, (rows, pages), 0) // length
            == lax.broadcasted_iota(jnp.int32, (rows, pages), 1),
            1.0,
            0.0,
        ).astype(jnp.bfloat16)
        tall = jnp.dot(spread, moves, preferred_element_type=jnp.float32).astype(jnp.bfloat16)
        wide = lax.dot_general(
            tall, spread, (((1,), (1,)), ((), ())), preferred_element_type=jnp.float32
        )
        full = (rows, rows)
        aligned = (
            lax.broadcasted_iota(jnp.int32, full, 0) % length
            == lax.broadcasted_iota(jnp.int32, full, 1) % length
        )
        mover = jnp.where(aligned, wide, 0.0).astype(jnp.bfloat16)
        strip = min(256, double)
        for c in range(double // strip):
            cols = slice(c * strip, (c + 1) * strip)
            outgoing[:, cols] = jnp.dot(
                mover, held[0, :, cols], preferred_element_type=jnp.float32
            ).astype(jnp.bfloat16)

    @pl.loop(0, LOOKBACK + 1)
    def _(t):
        @pl.when(t == 1)
        def _():
            order_pages()
            ahead(0).wait_recv()
            relay_ahead().start()
            for n in range(len(back)):
                backward(n).wait_recv()
                relay_back(n).start()

            for d in flat:
                page_copy(d).start()

            mine = pl.ds(pl.multiple_of(me * per, per), per)
            pltpu.make_async_copy(outgoing.at[mine], pages_ref.at[mine], local_sem.at[1]).start()
            ahead(1).wait_recv()

            @pl.when(core == 1)
            def _():
                beside(0).start()

            @pl.when(core == 0)
            def _():
                beside(1).start()

        @pl.when(t == 2)
        def _():
            beside(0).wait_recv()

        @pl.when(t == 3)
        def _():
            relay_ahead().wait_recv()
            for n in range(len(back)):
                relay_back(n).wait_recv()

            @pl.when(core == 1)
            def _():
                beside(1).start()

            fill()
            fill()

        @pl.when(t == 4)
        def _():
            beside(1).wait_recv()
            fill()

        offset = 0
        for n, value in enumerate((0, 2, 1, 4, 3)):
            offset = offset + jnp.where(t == n, value, 0)
        key_pos = (me - offset) * rows + lax.broadcasted_iota(jnp.int32, (1, rows), 1)
        for h in range(heads):
            keys[...] = held[offset, :, h * size : (h + 1) * size]
            values[...] = held[offset, :, width + h * size : width + (h + 1) * size]

            @pl.loop(0, rows // tile)
            def _(b, h=h):
                part = pl.ds(pl.multiple_of(b * tile, tile), tile)
                raw = lax.dot_general(
                    query[h, part, :],
                    keys[...],
                    (((1,), (1,)), ((), ())),
                    preferred_element_type=jnp.float32,
                )
                here = first_row + b * tile + lax.broadcasted_iota(jnp.int32, (tile, 1), 0)
                visible = (key_pos >= first_key[part, :]) & (key_pos <= here)
                scores = jnp.where(visible, raw * factor, -1e30)
                old = top[h, part, :]
                new = jnp.maximum(old, jnp.max(scores, axis=1, keepdims=True))
                terms = jnp.exp2(scores - new)
                shrink = jnp.exp2(old - new)
                weight[h, part, :] = weight[h, part, :] * shrink + jnp.sum(
                    terms, axis=1, keepdims=True
                )
                mixed[h, part, :] = mixed[h, part, :] * shrink + jnp.dot(
                    terms.astype(jnp.bfloat16), values[...], preferred_element_type=jnp.float32
                )
                top[h, part, :] = new

    for h in range(heads):
        out_ref[:, h * size : (h + 1) * size] = (mixed[h] / weight[h]).astype(jnp.bfloat16)
    requests = picked_ref.shape[0]
    which = lax.broadcasted_iota(jnp.int32, (requests, 1), 0)
    last = jnp.zeros((requests, 1), jnp.int32)
    for r in range(requests):
        end = 0
        for k in range(NPROMPT):
            end = end + jnp.where(request_ref[r] == k, bounds[k], 0)
        last = jnp.where(which == r, end - 1, last)
    chosen = jnp.where(
        last == first_row + lax.broadcasted_iota(jnp.int32, (requests, rows), 1), 1.0, 0.0
    ).astype(jnp.bfloat16)
    picked_ref[...] = jnp.dot(
        chosen, out_ref[...], preferred_element_type=jnp.float32
    ).astype(jnp.bfloat16)
    final_buf[...] = jnp.zeros_like(final_buf)
    last_tokens(
        ring,
        tps,
        fill,
        picked_ref,
        o_buf,
        gain_ref,
        un_buf,
        norm_ref,
        max_ref,
        row_a,
        row_b,
        row_sum,
        parts,
        states,
        final_buf,
        max_own,
        max_got,
        tail_send,
        tail_recv,
        load_o,
        load_u,
    )
    while waiting:
        fill()
    for n in range(2):
        ahead(n).wait_send()
        beside(n).wait_send()
    relay_ahead().wait_send()
    for n in range(len(back)):
        backward(n).wait_send()
        relay_back(n).wait_send()

    for batch in [flat] + batches:
        for d in batch:
            page_copy(d).wait()
    mine = pl.ds(pl.multiple_of(me * per, per), per)
    pltpu.make_async_copy(outgoing.at[mine], pages_ref.at[mine], local_sem.at[1]).wait()


def attend(
    lengths,
    req_prompt,
    page_owner,
    queries,
    local_rows,
    o_weight,
    final_gain,
    unembed,
    ring,
    tps,
):
    rows, width = queries.shape
    heads = width // HEAD
    count = 2 * ring * ring
    near = rows * 11 // 32
    third = (rows - near) // 3
    back = tuple((near + n * third, near + (n + 1) * third) for n in range(3))
    requests = req_prompt.shape[0]
    model = o_weight.shape[1]
    chunk = model // ring
    around, far = 2 * ring - 1, ring * tps - 1
    copies = 2 * around + far + 2 * (ring - 1) + tps - 1
    vmem = pl.BlockSpec(memory_space=pltpu.VMEM)
    smem = pl.BlockSpec(memory_space=pltpu.SMEM)
    anywhere = pl.BlockSpec(memory_space=pl.ANY)
    dma = pltpu.SemaphoreType.DMA
    attended, pages, norm, best = pl.pallas_call(
        functools.partial(attend_kernel, ring, tps, back),
        out_shape=(
            jax.ShapeDtypeStruct((rows, width), jnp.bfloat16),
            jax.ShapeDtypeStruct((rows, 2 * width), jnp.bfloat16),
            jax.ShapeDtypeStruct((requests, 128), jnp.float32),
            jax.ShapeDtypeStruct((8, 128), jnp.float32),
        ),
        in_specs=[smem, smem, vmem, vmem, anywhere, anywhere, vmem, anywhere],
        out_specs=(vmem, anywhere, vmem, vmem),
        scratch_shapes=[
            pltpu.VMEM((LOOKBACK + 1, rows, 2 * width), jnp.bfloat16),
            pltpu.VMEM((rows - near, 2 * width), jnp.bfloat16),
            pltpu.VMEM((rows, 2 * width), jnp.bfloat16),
            pltpu.VMEM((rows, HEAD), jnp.bfloat16),
            pltpu.VMEM((rows, HEAD), jnp.bfloat16),
            pltpu.VMEM((heads, rows, HEAD), jnp.bfloat16),
            pltpu.VMEM((heads, rows, HEAD), jnp.float32),
            pltpu.VMEM((heads, rows, 1), jnp.float32),
            pltpu.VMEM((heads, rows, 1), jnp.float32),
            pltpu.VMEM((rows, 1), jnp.int32),
            dma((2,)),
            dma((2,)),
            dma((3,)),
            dma((3,)),
            dma((4,)),
            dma((4,)),
            dma((2,)),
            dma((2,)),
            dma((count,)),
            dma((count,)),
            dma((4,)),
            pltpu.VMEM((requests, width), jnp.bfloat16),
            pltpu.VMEM((width, chunk), jnp.bfloat16),
            pltpu.VMEM(unembed.shape, jnp.bfloat16),
            pltpu.VMEM((around, requests, width), jnp.bfloat16),
            pltpu.VMEM((ring - 1, requests, width), jnp.bfloat16),
            pltpu.VMEM((requests, width), jnp.bfloat16),
            pltpu.VMEM((tps, requests, chunk), jnp.float32),
            pltpu.VMEM((ring, requests, chunk), jnp.float32),
            pltpu.VMEM((ring, 128, chunk), jnp.bfloat16),
            pltpu.VMEM((2, 8, 128), jnp.float32),
            pltpu.VMEM((around + far, 8, 128), jnp.float32),
            dma((copies,)),
            dma((copies,)),
        ],
        compiler_params=pltpu.CompilerParams(
            collective_id=2, has_side_effects=True, vmem_limit_bytes=60 << 20
        ),
        name="attend",
    )(
        lengths,
        req_prompt,
        page_owner.reshape(1, -1),
        queries,
        local_rows,
        o_weight,
        final_gain.reshape(1, model),
        unembed,
    )
    return attended, pages, norm[:, 0], best[0, :requests]


def local(
    hidden_cat,
    norm_gain,
    k_weight,
    v_weight,
    k_down,
    v_down,
    k_up,
    v_up,
    queries,
    o_weight,
    final_gain,
    unembed,
    lengths,
    req_prompt,
    page_owner,
):
    local_rows = project(
        hidden_cat, norm_gain, k_weight, v_weight, k_down, v_down, k_up, v_up, RING
    )
    attended, pages, state_norm, logit_max = attend(
        lengths,
        req_prompt,
        page_owner,
        queries,
        local_rows,
        o_weight,
        final_gain,
        unembed,
        RING,
        lax.axis_size("tp"),
    )
    rows, width = attended.shape
    kv_cache = pages.reshape(rows // PAGE, PAGE, 2, width)
    return (attended, kv_cache, state_norm, logit_max)


def solution(mesh):
    placed = (
        P("seq", None),
        P(),
        P("seq", "tp"),
        P("seq", "tp"),
        P("seq", None),
        P("seq", None),
        P(None, "tp"),
        P(None, "tp"),
        P("seq", "tp"),
        P("tp", None),
        P(),
        P(("seq", "tp"), None),
        P(),
        P(),
        P("seq"),
    )
    return jax.shard_map(
        local,
        mesh=mesh,
        in_specs=placed,
        out_specs=(P("seq", "tp"), P("seq", None, None, "tp"), P(), P()),
        check_vma=False,
    )
```
